32 devices in a mesh: prow: 4 (over y, core), pcol: 8 (over z, x).
Axes of the slice: x: 2, y: 2, z: 4, core: 2. Of those that a mesh axis runs over, the one named last changes fastest.
Arguments:
- covariance: bfloat16 [2, 4, 4, 512, 2, 8, 512], P(None, None, 'prow', None, None, 'pcol'), may hold values from 0 to 2, as said below
Outputs:
- factored: float32 [2, 4, 4, 512, 2, 8, 512], P(None, None, 'prow', None, None, 'pcol')
The draws below stay inside these ranges and needn't reach their ends.
Inputs may be any that keep to these rules, and one draw needn't show every extreme that they name: For each candidate a symmetric positive definite Matern covariance of scattered observations (smoothness 1/2, 3/2 or 5/2) plus a positive nugget on the diagonal.
All inputs are finite; a program needn't handle non-finite values.
Results may differ from the reference program's by a relative error of at most 0.0019.
Values may be sent and summed in bfloat16 or wider, within the bound.
A program may use at most 192 MiB of HBM per device.

```python
import math
import jax
import jax.numpy as jnp
from jax import lax

NB = 512
FACTORED = 2
CAND = 2
LC = 2
LR = 4
M = 8192


def draw_covariance(key, part):
    subkeys = jax.random.split(jax.random.fold_in(key, 11), 5)
    side_length = math.sqrt(M)
    coords = jax.random.uniform(subkeys[0], (CAND, 2, M), jnp.float32) * side_length
    length = side_length * jnp.exp(jax.random.uniform(subkeys[1], (CAND,), jnp.float32, math.log(0.08), math.log(0.25)))
    variance = jnp.exp(jax.random.uniform(subkeys[2], (CAND,), jnp.float32, math.log(0.7), math.log(1.4)))
    nugget = jax.random.uniform(subkeys[3], (CAND,), jnp.float32, 0.3, 0.5)
    smooth = jax.random.randint(subkeys[4], (CAND,), 0, 3)

    def one_block(block_index):
        first_row = block_index * NB
        near_points = lax.dynamic_slice_in_dim(coords, first_row, NB, 2)
        delta_x = near_points[:, 0, :, None] - coords[:, 0, None, :]
        delta_y = near_points[:, 1, :, None] - coords[:, 1, None, :]
        scaled = jnp.sqrt(delta_x * delta_x + delta_y * delta_y) / length[:, None, None]
        kernel_half = jnp.exp(-scaled)
        kernel_three = (1.0 + math.sqrt(3.0) * scaled) * jnp.exp(-math.sqrt(3.0) * scaled)
        kernel_five = (1.0 + math.sqrt(5.0) * scaled + 5.0 * scaled * scaled / 3.0) * jnp.exp(-math.sqrt(5.0) * scaled)
        code = smooth[:, None, None]
        kernel = jnp.where(code == 0, kernel_half, jnp.where(code == 1, kernel_three, kernel_five))
        same_point = (first_row + jnp.arange(NB))[:, None] == jnp.arange(M)[None, :]
        entries = variance[:, None, None] * kernel + jnp.where(same_point[None], nugget[:, None, None], 0.0)
        return entries.astype(jnp.bfloat16)
    stacked = lax.map(one_block, jnp.arange(M // NB))
    whole = jnp.transpose(stacked, (1, 0, 2, 3)).reshape(CAND, M, M)
    return whole.reshape(CAND, LR, M // (LR * NB), NB, LC, M // (LC * NB), NB)


def setup_inputs(seed: int = 0) -> dict:
    arg_keys = jax.random.split(jax.random.key(seed), 2)
    return {
        "covariance": draw_covariance(jax.random.fold_in(arg_keys[1], 71), 0),
    }


def factor_one(matrix):
    matrix = matrix.astype(jnp.float32)
    row_index = jnp.arange(M)
    columns = []
    for tile_step in range(FACTORED):
        start_row = tile_step * NB
        diag_block = matrix[start_row:start_row + NB, start_row:start_row + NB]
        lower_factor = jnp.linalg.cholesky(diag_block)
        solved = lax.linalg.triangular_solve(lower_factor, matrix[:, start_row:start_row + NB], left_side=False, lower=True, transpose_a=True)
        below_mask = (row_index >= start_row + NB)[:, None]
        panel_rows = jnp.where(below_mask, solved, 0.0)
        columns.append(panel_rows.at[start_row:start_row + NB].set(lower_factor))
        rounded = panel_rows.astype(jnp.bfloat16)
        matrix = matrix - jnp.dot(rounded.astype(jnp.float32), rounded.T.astype(jnp.float32), preferred_element_type=jnp.float32)
    factored_cols = FACTORED * NB
    upper_mask = (row_index < factored_cols)[:, None]
    right_part = jnp.where(upper_mask, 0.0, matrix[:, factored_cols:])
    return jnp.concatenate(columns + [right_part], axis=1)

def reference(covariance):
    whole = covariance.reshape(CAND, M, M)
    result = jnp.stack([factor_one(whole[candidate]) for candidate in range(CAND)])
    return result.reshape(covariance.shape)
```

```python
import functools

import jax
import jax.numpy as jnp
from jax import lax
from jax.experimental import pallas as pl
from jax.experimental.pallas import tpu as pltpu
from jax.sharding import PartitionSpec as P

FACTORED = 2
BLOCK = 128
STRIP = 8
LANES = 128
ROWS = 256
TILES = ((0, 0), (0, 1), (1, 1))
HIGH = lax.Precision.HIGHEST
MESH = pl.DeviceIdType.MESH
F32 = jnp.float32
BF16 = jnp.bfloat16


def mm(a, b):
    return jnp.dot(a, b, preferred_element_type=F32)


def mm_nt(a, b):
    return lax.dot_general(a, b, (((1,), (1,)), ((), ())), preferred_element_type=F32)


def mm_tn(a, b):
    return lax.dot_general(a, b, (((0,), (0,)), ((), ())), preferred_element_type=F32)


def dot_t(a, b):
    return lax.dot_general(a, b, (((0,), (0,)), ((), ())), precision=HIGH, preferred_element_type=F32)


def split(value):
    high = value.astype(BF16)
    return high, (value - high.astype(F32)).astype(BF16)


def factor(load, upper_ref, inverse_ref, work, diag, cands, side, slot):
    blocks = side // BLOCK
    strips_per_block = BLOCK // STRIP
    eye_row = lax.broadcasted_iota(jnp.int32, (BLOCK, BLOCK), 0)
    eye_col = lax.broadcasted_iota(jnp.int32, (BLOCK, BLOCK), 1)
    eye = (eye_row == eye_col).astype(F32)
    sub_narrow = lax.broadcasted_iota(jnp.int32, (STRIP, BLOCK), 0)
    sub_wide = lax.broadcasted_iota(jnp.int32, (STRIP, 2 * BLOCK), 0)
    lane = lax.broadcasted_iota(jnp.int32, (STRIP, BLOCK), 1)
    for c in range(cands):
        work[c, :, side:] = jnp.zeros((side, side), F32)
        for block in range(blocks):
            lo = block * BLOCK
            if lo:
                work[c, lo : lo + BLOCK, :lo] = jnp.zeros((BLOCK, lo), F32)
            work[c, lo : lo + BLOCK, lo:side] = load(c, lo)
            work[c, lo : lo + BLOCK, side + lo : side + lo + BLOCK] = eye
    for block in range(blocks):
        lo = block * BLOCK
        hi = lo + BLOCK
        for c in range(cands):
            diag[c, :, :BLOCK] = work[c, lo:hi, lo:hi]
            diag[c, :, BLOCK:] = eye

        def strip_step(step, carry):
            slot(block * strips_per_block + step)
            start = pl.multiple_of(step * STRIP, STRIP)
            strips = [diag[c, pl.ds(start, STRIP), :] for c in range(cands)]
            turned = [
                pltpu.roll(strip[:, :BLOCK], lax.rem(BLOCK - start, BLOCK), 1) for strip in strips
            ]
            for t in range(STRIP):
                for c in range(cands):
                    column = jnp.broadcast_to(turned[c][:, t : t + 1], (STRIP, BLOCK))
                    scale = lax.rsqrt(jnp.broadcast_to(column[t : t + 1], (STRIP, BLOCK)))
                    factor = column * (scale * scale)
                    wide_factor = jnp.concatenate([factor, factor], axis=1)
                    wide_scale = jnp.concatenate([scale, scale], axis=1)
                    row = turned[c][t : t + 1]
                    wide_row = strips[c][t : t + 1]
                    turned[c] = jnp.where(sub_narrow > t, turned[c] - factor * row, turned[c])
                    strips[c] = jnp.where(
                        sub_wide > t,
                        strips[c] - wide_factor * wide_row,
                        jnp.where(sub_wide == t, strips[c] * wide_scale, strips[c]),
                    )
            for c in range(cands):
                diag[c, pl.ds(start, STRIP), :] = strips[c]
            for c in range(cands):
                later = jnp.where(lane >= start + STRIP, strips[c][:, :BLOCK], 0.0)
                diag[c] = diag[c] - dot_t(later, strips[c])
            return carry

        lax.fori_loop(0, strips_per_block, strip_step, 0)
        for c in range(cands):
            small = jnp.where(eye_row >= eye_col, diag[c, :, BLOCK:], 0.0)
            done = jnp.dot(
                small, work[c, lo:hi, lo : side + hi], precision=HIGH, preferred_element_type=F32
            )
            upper_ref[c, lo:hi, lo:side] = done[:, : side - lo]
            upper_ref[c, lo:hi, lo:hi] = jnp.where(eye_row <= eye_col, diag[c, :, :BLOCK], 0.0)
            if lo:
                upper_ref[c, lo:hi, :lo] = jnp.zeros((BLOCK, lo), F32)
            inverse_ref[c, lo:hi, :hi] = done[:, side - lo :]
            if hi < side:
                inverse_ref[c, lo:hi, hi:] = jnp.zeros((BLOCK, side - hi), F32)
                work[c, hi:, hi : side + hi] = work[c, hi:, hi : side + hi] - dot_t(
                    done[:, BLOCK : side - lo], done[:, BLOCK:]
                )


def head_kernel(
    prows, pcols, base, upper0, inverse0, upper1, inverse1, near, rows_out, cols_out,
    work, diag, tiles, rows, cols,
    tile_recv, tile_send, row_recv, row_send, col_recv, col_send, row_flush, col_flush,
):
    cands, side = upper0.shape[:2]
    blocks = side // BLOCK
    p, q = lax.axis_index("prow"), lax.axis_index("pcol")
    y, core, z, x = p // 2, p % 2, q // 2, q % 2
    lines, planes = pcols // 2, prows // 2
    row_chunks, row_size = rows.shape[1:3]
    col_chunks, col_size = cols.shape[1:3]
    per_row = row_chunks // cands
    per_col = col_chunks // cands

    def at(dy=None, dcore=None, dz=None, dx=None):
        pick = lambda new, old: old if new is None else new
        return {
            "prow": pick(dy, y) * 2 + pick(dcore, core),
            "pcol": pick(dz, z) * 2 + pick(dx, x),
        }

    barrier = pltpu.get_barrier_semaphore()
    for target in (
        at(dy=(y + 1) % planes), at(dy=(y + planes - 1) % planes), at(dcore=1 - core),
        at(dz=(z + 1) % lines), at(dz=(z + lines - 1) % lines), at(dx=1 - x),
    ):
        pl.semaphore_signal(barrier, inc=1, device_id=target, device_id_type=MESH)

    def tile_part(tile, index):
        c, lo = index % cands, index // cands * BLOCK
        first = 0 if tile == 1 else lo
        return c, slice(lo, lo + BLOCK), slice(first, side)

    tile_count = cands * blocks

    def row_source(i):
        start = pl.multiple_of(i % per_row * row_size, row_size)
        return base.at[i // per_row, pl.ds(start, row_size), :side]

    def row_target(k, i):
        start = pl.multiple_of(i % per_row * row_size, row_size)
        return rows_out.at[k, i // per_row, pl.ds(start, row_size)]

    def col_source(i):
        start = pl.multiple_of(i % per_col * col_size, col_size)
        return base.at[i // per_col, pl.ds(start, col_size)]

    def col_target(k, i):
        start = pl.multiple_of(i % per_col * col_size, col_size)
        return cols_out.at[k, i // per_col, pl.ds(start, col_size)]

    for tile, (p0, q0) in enumerate(TILES):
        @pl.when((p == p0) & (q == q0))
        def _():
            for index in range(tile_count):
                c, r, s = tile_part(tile, index)
                pltpu.make_async_copy(base.at[c, r, s], tiles.at[tile, c, r, s], tile_recv.at[tile, index]).start()

    @pl.when(z == 0)
    def _():
        @pl.loop(0, row_chunks)
        def _(i):
            pltpu.make_async_copy(row_source(i), rows.at[x, i], row_recv.at[x, i]).start()

    @pl.when(y == 0)
    def _():
        @pl.loop(0, col_chunks)
        def _(i):
            pltpu.make_async_copy(col_source(i), cols.at[core, i], col_recv.at[core, i]).start()

    pl.semaphore_wait(barrier, 6)

    def tile_sends(tile, index):
        p0, q0 = TILES[tile]
        c, r, s = tile_part(tile, index)
        ref = tiles.at[tile, c, r, s]
        even = core == 0
        line = even & (x == q0)
        source = (p == p0) & (q == q0)
        partner = (y == 0) & (1 - core == p0) & (q == q0)
        options = [
            (line & (z < lines - 1), at(dz=z + 1)),
            (line & (z == 0) & (y < planes - 1), at(dy=y + 1)),
            (line, at(dx=1 - x)),
            ((even & jnp.logical_not(partner)) | ((core == 1) & source), at(dcore=1 - core)),
        ]
        return [
            (
                condition,
                pltpu.make_async_remote_copy(
                    src_ref=ref, dst_ref=ref, send_sem=tile_send.at[tile, index, way],
                    recv_sem=tile_recv.at[tile, index], device_id=target, device_id_type=MESH,
                ),
            )
            for way, (condition, target) in enumerate(options)
        ]

    def tile_relay(tile, index):
        c, r, s = tile_part(tile, index)
        ref = tiles.at[tile, c, r, s]
        pltpu.make_async_copy(ref, ref, tile_recv.at[tile, index]).wait()
        for condition, copy in tile_sends(tile, index):
            pl.when(condition)(copy.start)

    def sends(buffer, i, k, send, recv, more, step, side_step):
        ref = buffer.at[k, i]
        copy = lambda way, target: pltpu.make_async_remote_copy(
            src_ref=ref, dst_ref=ref, send_sem=send.at[way, i], recv_sem=recv.at[k, i],
            device_id=target, device_id_type=MESH,
        )
        return [(more, copy(0, step)), (None, copy(1, side_step))]

    def row_sends(i):
        return sends(rows, i, x, row_send, row_recv, z < lines - 1, at(dz=jnp.minimum(z + 1, lines - 1)), at(dx=1 - x))

    def col_sends(i):
        return sends(cols, i, core, col_send, col_recv, y < planes - 1, at(dy=jnp.minimum(y + 1, planes - 1)), at(dcore=1 - core))

    def begin(options):
        for condition, copy in options:
            if condition is None:
                copy.start()
            else:
                pl.when(condition)(copy.start)

    def finish(options):
        for condition, copy in options:
            if condition is None:
                copy.wait_send()
            else:
                pl.when(condition)(copy.wait_send)

    def row_land(k, i):
        pltpu.make_async_copy(rows.at[k, i], rows.at[k, i], row_recv.at[k, i]).wait()
        pltpu.make_async_copy(rows.at[k, i], row_target(k, i), row_flush.at[k, i]).start()

    def col_land(k, i):
        pltpu.make_async_copy(cols.at[k, i], cols.at[k, i], col_recv.at[k, i]).wait()
        pltpu.make_async_copy(cols.at[k, i], col_target(k, i), col_flush.at[k, i]).start()

    def row_slot(i):
        @pl.when((i >= 0) & (i < row_chunks))
        def _():
            row_land(x, i)
            begin(row_sends(i))

        @pl.when((i >= 2) & (i < row_chunks + 2))
        def _():
            row_land(1 - x, i - 2)

    def col_slot(i):
        @pl.when((i >= 0) & (i < col_chunks))
        def _():
            col_land(core, i)
            begin(col_sends(i))

        @pl.when((i >= 2) & (i < col_chunks + 2))
        def _():
            col_land(1 - core, i - 2)

    for index in range(tile_count):
        tile_relay(0, index)
    for index in range(tile_count):
        tile_relay(1, index)
    for index in range(tile_count):
        tile_relay(2, index)

    strips = side // STRIP

    def slot_of(offset):
        def slot(step):
            n = offset + step

            @pl.when(n % 2 == 0)
            def _():
                row_slot(n // 2 - z)

            @pl.when(n % 2 == 1)
            def _():
                col_slot(n // 2 - y)

        return slot

    factor(
        lambda c, lo: tiles[0, c, lo : lo + BLOCK, lo:].astype(F32),
        upper0, inverse0, work, diag, cands, side, slot_of(0),
    )
    for c in range(cands):
        inv = inverse0[c]
        a = inv.astype(BF16)
        rest = inv - a.astype(F32)
        b = rest.astype(BF16)
        d = (rest - b.astype(F32)).astype(BF16)
        raw = tiles[1, c]
        near[c] = (mm(d, raw) + mm(b, raw) + mm(a, raw)).astype(BF16)
        work[c, :, :side] = mm_tn(near[c], near[c])
    factor(
        lambda c, lo: tiles[2, c, lo : lo + BLOCK, lo:].astype(F32) - work[c, lo : lo + BLOCK, lo:side],
        upper1, inverse1, work, diag, cands, side, slot_of(strips),
    )

    reached = strips

    @pl.loop(0, row_chunks + 2)
    def _(i):
        @pl.when(i > reached - 1 - z)
        def _():
            row_slot(i)

    @pl.loop(0, col_chunks + 2)
    def _(i):
        @pl.when(i > reached - 1 - y)
        def _():
            col_slot(i)

    for tile in range(len(TILES)):
        for index in range(tile_count):
            finish(tile_sends(tile, index))

    @pl.loop(0, row_chunks)
    def _(i):
        finish(row_sends(i))
        for k in range(FACTORED):
            pltpu.make_async_copy(rows.at[k, i], row_target(k, i), row_flush.at[k, i]).wait()

    @pl.loop(0, col_chunks)
    def _(i):
        finish(col_sends(i))
        for k in range(FACTORED):
            pltpu.make_async_copy(cols.at[k, i], col_target(k, i), col_flush.at[k, i]).wait()


def head(prows, pcols, side, base):
    cands, row_count, columns = base.shape
    square = jax.ShapeDtypeStruct((cands, side, side), F32)
    vmem = pl.BlockSpec(memory_space=pltpu.VMEM)
    hbm = pl.BlockSpec(memory_space=pl.ANY)
    dma = pltpu.SemaphoreType.DMA
    row_chunks = cands * row_count // ROWS
    col_chunks = cands * side // BLOCK
    count = cands * side // BLOCK
    return pl.pallas_call(
        functools.partial(head_kernel, prows, pcols),
        out_shape=(
            square, square, square, square, jax.ShapeDtypeStruct((cands, side, side), BF16),
            jax.ShapeDtypeStruct((FACTORED, cands, row_count, side), BF16),
            jax.ShapeDtypeStruct((FACTORED, cands, side, columns), BF16),
        ),
        in_specs=[hbm],
        out_specs=(vmem,) * 5 + (hbm, hbm),
        scratch_shapes=[
            pltpu.VMEM((cands, side, 2 * side), F32),
            pltpu.VMEM((cands, BLOCK, 2 * BLOCK), F32),
            pltpu.VMEM((len(TILES), cands, side, side), BF16),
            pltpu.VMEM((FACTORED, row_chunks, ROWS, side), BF16),
            pltpu.VMEM((FACTORED, col_chunks, BLOCK, columns), BF16),
            dma((len(TILES), count)), dma((len(TILES), count, 4)),
            dma((FACTORED, row_chunks)), dma((2, row_chunks)),
            dma((FACTORED, col_chunks)), dma((2, col_chunks)),
            dma((FACTORED, row_chunks)), dma((FACTORED, col_chunks)),
        ],
        compiler_params=pltpu.CompilerParams(collective_id=0, has_side_effects=True, vmem_limit_bytes=60 << 20),
        cost_estimate=pl.CostEstimate(flops=40_000_000_000, bytes_accessed=1 << 25, transcendentals=0),
        name="head",
    )(base)


def tail_kernel(prows, pcols, place, base, rows_ref, cols_ref, upper0, upper1, inv0, inv1, near, out, cols, parts):
    side = inv0.shape[-1]
    half = side // 2
    columns = base.shape[-1]
    block = pl.program_id(1)
    p, q = place[0], place[1]
    tile = block * ROWS // side * prows + p

    @pl.when(block == 0)
    def _():
        for index, inv in enumerate((inv0, inv1)):
            high, low = split(inv[0])
            parts[2 * index] = high
            parts[2 * index + 1] = low
        for index in range(columns // side):
            at = slice(index * side, (index + 1) * side)
            column = index * pcols + q
            raw = cols_ref[0, 0, :, at]
            solved = mm(parts[0], raw) + mm(parts[1], raw)
            first = jnp.where(column > 0, solved, 0.0).astype(BF16)
            cols[:side, at] = first
            rest = cols_ref[1, 0, :, at].astype(F32) - lax.dot_general(
                near[0], first, (((0,), (0,)), ((), ())), preferred_element_type=F32)
            high, low = split(rest)
            solved = mm(parts[2], high) + (mm(parts[3], high) + mm(parts[2], low))
            cols[side:, at] = jnp.where(column > 1, solved, 0.0).astype(BF16)

    def solve(pairs):
        left = sum(mm_nt(a[:, :half], b[:half, :half]) for a, b in pairs)
        right = sum(mm_nt(a, b[half:, :]) for a, b in pairs)
        return jnp.concatenate([left, right], axis=1)

    raw = rows_ref[0, 0]
    solved0 = solve([(raw, parts[0]), (raw, parts[1])])
    solved0 = jnp.where(tile > 0, solved0, 0.0)
    first = solved0.astype(BF16)
    rest = rows_ref[1, 0].astype(F32) - mm(first, near[0])
    high, low = split(rest)
    solved1 = solve([(high, parts[2]), (high, parts[3]), (low, parts[2])])
    solved1 = jnp.where(tile > 1, solved1, 0.0)
    second = solved1.astype(BF16)
    wide = columns // LANES
    rows = pl.ds(pl.multiple_of(lax.rem(block * ROWS, side), ROWS), ROWS)

    def store(value, start):
        for lane in range(value.shape[1] // LANES):
            out[pl.ds(start // LANES + lane, ROWS, stride=wide), :] = value[:, lane * LANES : (lane + 1) * LANES]

    def trail(start):
        at = slice(start, start + half)
        value = base[0, :, at].astype(F32) - (mm(first, cols[:side, at]) + mm(second, cols[side:, at]))
        store(jnp.where(tile > 1, value, 0.0), start)

    for start in range(side, columns, half):
        trail(start)

    @pl.when(q > 1)
    def _():
        for start in range(0, side, half):
            trail(start)

    for k, (solved, upper) in enumerate(((solved0, upper0), (solved1, upper1))):
        @pl.when(q == k)
        def _():
            store(solved, 0)

            @pl.when(tile == k)
            def _():
                store(upper[0, :, rows].T, 0)


def tail(prows, pcols, place, base, rows_in, cols_in, upper0, upper1, inv0, inv1, near):
    cands, rows, columns = base.shape
    side = inv0.shape[-1]
    whole = lambda a: pl.BlockSpec((1,) + a.shape[1:], lambda c, b, s: (c, 0, 0))
    part = lambda a: pl.BlockSpec((1, ROWS, a.shape[2]), lambda c, b, s: (c, b, 0))
    wide = columns // LANES
    return pl.pallas_call(
        functools.partial(tail_kernel, prows, pcols),
        out_shape=jax.ShapeDtypeStruct((cands * rows * wide, LANES), F32),
        grid_spec=pltpu.PrefetchScalarGridSpec(
            num_scalar_prefetch=1,
            grid=(cands, rows // ROWS),
            in_specs=[
                part(base),
                pl.BlockSpec((FACTORED, 1, ROWS, side), lambda c, b, s: (0, c, b, 0)),
                pl.BlockSpec((FACTORED, 1, side, columns), lambda c, b, s: (0, c, 0, 0)),
            ]
            + [whole(a) for a in (upper0, upper1, inv0, inv1, near)],
            out_specs=pl.BlockSpec((ROWS * wide, LANES), lambda c, b, s: (c * (rows // ROWS) + b, 0)),
            scratch_shapes=[pltpu.VMEM((2 * side, columns), BF16), pltpu.VMEM((4, side, side), BF16)],
        ),
        cost_estimate=pl.CostEstimate(flops=2 * cands * rows * columns * 2 * side, bytes_accessed=cands * rows * columns * 6, transcendentals=0),
        name="tail",
    )(place, base, rows_in, cols_in, upper0, upper1, inv0, inv1, near)


def shards(covariance):
    cands, row_tiles, _, side, column_tiles = covariance.shape[:5]
    prows = lax.axis_size("prow")
    pcols = lax.axis_size("pcol")
    place = jnp.stack([lax.axis_index("prow"), lax.axis_index("pcol")]).astype(jnp.int32)
    base = covariance.reshape(cands, row_tiles * side, column_tiles * side)
    upper0, inverse0, upper1, inverse1, near, rows, cols = head(prows, pcols, side, base)
    out = tail(prows, pcols, place, base, rows, cols, upper0, upper1, inverse0, inverse1, near)
    return out.reshape(covariance.shape)


def solution(mesh):
    placed = P(None, None, "prow", None, None, "pcol", None)
    return jax.shard_map(
        shards, mesh=mesh, in_specs=(placed,), out_specs=placed, check_vma=False
    )
```

```python
import functools

import jax
import jax.numpy as jnp
from jax import lax
from jax.experimental import pallas as pl
from jax.experimental.pallas import tpu as pltpu
from jax.sharding import PartitionSpec as P

FACTORED = 2
ROW_START, ROW_LATER, ROW_HOP, ROW_PACE, AHEAD = 4, 15, 2, 3, 2
COL_START, BETWEEN = 30, 4
TILE_START = (0, 5, 17)
BLOCK = 128
STRIP = 16
HALF = 8
LANES = 128
ROWS = 256
TILES = ((0, 0), (0, 1), (1, 1))
MESH = pl.DeviceIdType.MESH
F32 = jnp.float32
BF16 = jnp.bfloat16


def mm(a, b):
    return jnp.dot(a, b, preferred_element_type=F32)


def mm_nt(a, b):
    return lax.dot_general(a, b, (((1,), (1,)), ((), ())), preferred_element_type=F32)


def mm_tn(a, b):
    return lax.dot_general(a, b, (((0,), (0,)), ((), ())), preferred_element_type=F32)


def split(value):
    high = value.astype(BF16)
    return high, (value - high.astype(F32)).astype(BF16)


def thirds(value):
    a = value.astype(BF16)
    rest = value - a.astype(F32)
    b = rest.astype(BF16)
    return a, b, (rest - b.astype(F32)).astype(BF16)


def dot6(left, right, turned=False):
    a, b, c = thirds(left)
    d, e, f = thirds(right)
    lefts = jnp.concatenate([a, a, b, a, c, b], 0 if turned else 1)
    rights = jnp.concatenate([d, e, d, f, d, e], 0)
    return (mm_tn if turned else mm)(lefts, rights)


def row_of(value, index):
    return jnp.broadcast_to(value[index : index + 1], value.shape)


def small_inverse(columns):
    n = len(columns)
    d = [[row_of(columns[t], i) if i >= t else None for t in range(n)] for i in range(n)]
    m = [[None] * n for _ in range(n)]
    sums = [[None] * n for _ in range(n)]
    for t in range(n):
        scale = lax.rsqrt(d[t][t])
        for j in range(t):
            m[t][j] = -(scale * sums[t][j])
        m[t][t] = scale
        for i in range(t + 1, n):
            d[i][t] = d[i][t] * scale
        for i in range(t + 1, n):
            for j in range(t + 1, i + 1):
                d[i][j] = d[i][j] - d[i][t] * d[j][t]
        for i in range(t + 1, n):
            for j in range(t + 1):
                term = d[i][t] * m[t][j]
                sums[i][j] = term if sums[i][j] is None else sums[i][j] + term
    return m


def factor(load, upper_ref, inverse_ref, work, diag, done_ref, cands, side, slot):
    blocks = side // BLOCK
    strips_per_block = BLOCK // STRIP
    eye_row = lax.broadcasted_iota(jnp.int32, (BLOCK, BLOCK), 0)
    eye_col = lax.broadcasted_iota(jnp.int32, (BLOCK, BLOCK), 1)
    eye = (eye_row == eye_col).astype(F32)
    sub = lax.broadcasted_iota(jnp.int32, (HALF, BLOCK), 0)
    each = range(cands)
    for c in each:
        work[c, :, side:] = jnp.zeros((side, side), F32)
        for block in range(blocks):
            lo = block * BLOCK
            if lo:
                work[c, lo : lo + BLOCK, :lo] = jnp.zeros((BLOCK, lo), F32)
            work[c, lo : lo + BLOCK, lo:side] = load(c, lo)
            work[c, lo : lo + BLOCK, side + lo : side + lo + BLOCK] = eye

    def spread(value, start):
        return [jnp.broadcast_to(value[:, start + t : start + t + 1], (HALF, BLOCK)) for t in range(HALF)]

    def apply(m, rows):
        out = None
        for j in range(HALF):
            column = m[j][j] if j == 0 else jnp.where(sub == j, m[j][j], 0.0)
            for i in range(j + 1, HALF):
                column = jnp.where(sub == i, m[i][j], column)
            term = jnp.concatenate([column, column], axis=1) * row_of(rows, j)
            out = term if out is None else out + term
        return out

    for block in range(blocks):
        lo = block * BLOCK
        hi = lo + BLOCK
        for c in each:
            diag[c, :, :BLOCK] = work[c, lo:hi, lo:hi]
            diag[c, :, BLOCK:] = eye

        def strip_step(step, carry):
            slot(block * strips_per_block + step)
            start = pl.multiple_of(step * STRIP, STRIP)
            shift = lax.rem(BLOCK - start, BLOCK)
            top = [diag[c, pl.ds(start, HALF), :] for c in each]
            low = [diag[c, pl.ds(start + HALF, HALF), :] for c in each]
            top_columns = [spread(pltpu.roll(top[c][:, :BLOCK], shift, 1), 0) for c in each]
            low_columns = [spread(pltpu.roll(low[c][:, :BLOCK], shift, 1), 0) for c in each]
            m = [small_inverse(top_columns[c]) for c in each]
            first = [apply(m[c], top[c]) for c in each]
            rest = []
            for c in each:
                value = low[c]
                for j in range(HALF):
                    left = sum(m[c][j][t] * low_columns[c][t] for t in range(j + 1))
                    value = value - jnp.concatenate([left, left], axis=1) * row_of(first[c], j)
                rest.append(value)
            last_columns = [spread(pltpu.roll(rest[c][:, :BLOCK], shift, 1), HALF) for c in each]
            m = [small_inverse(last_columns[c]) for c in each]
            second = [apply(m[c], rest[c]) for c in each]
            for c in each:
                both = jnp.concatenate([first[c], second[c]], axis=0)
                done_ref[c, pl.ds(start, STRIP), :] = both
                diag[c] = diag[c] - dot6(both[:, :BLOCK], both, turned=True)
            return carry

        lax.fori_loop(0, strips_per_block, strip_step, 0)
        for c in each:
            small = jnp.where(eye_row >= eye_col, done_ref[c, :, BLOCK:], 0.0)
            done = dot6(small, work[c, lo:hi, lo : side + hi])
            upper_ref[c, lo:hi, lo:side] = done[:, : side - lo]
            upper_ref[c, lo:hi, lo:hi] = jnp.where(eye_row <= eye_col, done_ref[c, :, :BLOCK], 0.0)
            if lo:
                upper_ref[c, lo:hi, :lo] = jnp.zeros((BLOCK, lo), F32)
            inverse_ref[c, lo:hi, :hi] = done[:, side - lo :]
            if hi < side:
                inverse_ref[c, lo:hi, hi:] = jnp.zeros((BLOCK, side - hi), F32)
                work[c, hi:, hi : side + hi] = work[c, hi:, hi : side + hi] - dot6(
                    done[:, BLOCK : side - lo], done[:, BLOCK:], turned=True
                )


def head_kernel(
    prows, pcols, base, upper0, inverse0, upper1, inverse1, near, rows_out, cols_out,
    work, diag, done, tiles, rows, cols,
    tile_recv, tile_send, row_recv, row_send, col_recv, col_send, row_flush, col_flush,
):
    cands, side = upper0.shape[:2]
    blocks = side // BLOCK
    p, q = lax.axis_index("prow"), lax.axis_index("pcol")
    y, core, z, x = p // 2, p % 2, q // 2, q % 2
    lines, planes = pcols // 2, prows // 2
    row_chunks, row_size = rows.shape[1:3]
    col_chunks, col_size = cols.shape[1:3]
    per_row = row_chunks // cands
    per_col = col_chunks // cands

    def at(dy=None, dcore=None, dz=None, dx=None):
        pick = lambda new, old: old if new is None else new
        return {
            "prow": pick(dy, y) * 2 + pick(dcore, core),
            "pcol": pick(dz, z) * 2 + pick(dx, x),
        }

    barrier = pltpu.get_barrier_semaphore()
    for target in (
        at(dy=(y + 1) % planes), at(dy=(y + planes - 1) % planes), at(dcore=1 - core),
        at(dz=(z + 1) % lines), at(dz=(z + lines - 1) % lines), at(dx=1 - x),
    ):
        pl.semaphore_signal(barrier, inc=1, device_id=target, device_id_type=MESH)

    def tile_part(tile, index):
        c, lo = index % cands, index // cands * BLOCK
        if tile:
            return c, pl.ds(pl.multiple_of(lo, BLOCK), BLOCK), slice(0, side)
        return c, slice(lo, lo + BLOCK), slice(lo, side)

    tile_count = cands * blocks

    def row_source(i):
        start = pl.multiple_of(i % per_row * row_size, row_size)
        return base.at[i // per_row, pl.ds(start, row_size), :side]

    def row_target(k, i):
        start = pl.multiple_of(i % per_row * row_size, row_size)
        return rows_out.at[k, i // per_row, pl.ds(start, row_size)]

    def col_source(i):
        start = pl.multiple_of(i % per_col * col_size, col_size)
        return base.at[i // per_col, pl.ds(start, col_size)]

    def col_target(k, i):
        start = pl.multiple_of(i % per_col * col_size, col_size)
        return cols_out.at[k, i // per_col, pl.ds(start, col_size)]

    for tile, (p0, q0) in enumerate(TILES):
        @pl.when((p == p0) & (q == q0))
        def _():
            for index in range(tile_count):
                c, r, s = tile_part(tile, index)
                pltpu.make_async_copy(base.at[c, r, s], tiles.at[tile, c, r, s], tile_recv.at[tile, index]).start()

    @pl.when(z == 0)
    def _():
        @pl.loop(0, row_chunks)
        def _(i):
            pltpu.make_async_copy(row_source(i), rows.at[x, i], row_recv.at[x, i]).start()

    @pl.when(y == 0)
    def _():
        @pl.loop(0, col_chunks)
        def _(i):
            pltpu.make_async_copy(col_source(i), cols.at[core, i], col_recv.at[core, i]).start()

    pl.semaphore_wait(barrier, 6)

    def tile_sends(tile, index):
        p0, q0 = TILES[tile]
        c, r, s = tile_part(tile, index)
        ref = tiles.at[tile, c, r, s]
        even = core == 0
        line = even & (y == 0) & (x == q0)
        source = (p == p0) & (q == q0)
        partner = (y == 0) & (1 - core == p0) & (q == q0)
        options = [
            (line & (z < lines - 1), at(dz=z + 1)),
            (even & (y < planes - 1), at(dy=y + 1)),
            (line, at(dx=1 - x)),
            ((even & jnp.logical_not(partner)) | ((core == 1) & source), at(dcore=1 - core)),
        ]
        return [
            (
                condition,
                pltpu.make_async_remote_copy(
                    src_ref=ref, dst_ref=ref, send_sem=tile_send.at[tile, index, way],
                    recv_sem=tile_recv.at[tile, index], device_id=target, device_id_type=MESH,
                ),
            )
            for way, (condition, target) in enumerate(options)
        ]

    def tile_relay(tile, index):
        c, r, s = tile_part(tile, index)
        ref = tiles.at[tile, c, r, s]
        pltpu.make_async_copy(ref, ref, tile_recv.at[tile, index]).wait()
        for condition, copy in tile_sends(tile, index):
            pl.when(condition)(copy.start)

    def sends(buffer, i, k, send, recv, more, step, side_step):
        ref = buffer.at[k, i]
        copy = lambda way, target: pltpu.make_async_remote_copy(
            src_ref=ref, dst_ref=ref, send_sem=send.at[way, i], recv_sem=recv.at[k, i],
            device_id=target, device_id_type=MESH,
        )
        return [(more, copy(0, step)), (None, copy(1, side_step))]

    def row_sends(i):
        return sends(rows, i, x, row_send, row_recv, z < lines - 1, at(dz=jnp.minimum(z + 1, lines - 1)), at(dx=1 - x))

    def col_sends(i):
        return sends(cols, i, core, col_send, col_recv, y < planes - 1, at(dy=jnp.minimum(y + 1, planes - 1)), at(dcore=1 - core))

    def begin(options):
        for condition, copy in options:
            if condition is None:
                copy.start()
            else:
                pl.when(condition)(copy.start)

    def finish(options):
        for condition, copy in options:
            if condition is None:
                copy.wait_send()
            else:
                pl.when(condition)(copy.wait_send)

    def row_land(k, i):
        pltpu.make_async_copy(rows.at[k, i], rows.at[k, i], row_recv.at[k, i]).wait()
        pltpu.make_async_copy(rows.at[k, i], row_target(k, i), row_flush.at[k, i]).start()

    def col_land(k, i):
        pltpu.make_async_copy(cols.at[k, i], cols.at[k, i], col_recv.at[k, i]).wait()
        pltpu.make_async_copy(cols.at[k, i], col_target(k, i), col_flush.at[k, i]).start()

    skipped = (1 - jnp.minimum(y, 1)) * (side // row_size)
    stream = per_row - skipped
    row_total = cands * stream

    def chunk_of(j):
        return j // stream * per_row + skipped + j % stream

    def row_line(j):
        @pl.when((j >= 0) & (j < row_total))
        def _():
            i = chunk_of(j)
            row_land(x, i)
            begin(row_sends(i))

    def row_side(j):
        @pl.when((j >= 0) & (j < row_total))
        def _():
            row_land(1 - x, chunk_of(j))

    def col_line(i):
        @pl.when((i >= 0) & (i < col_chunks))
        def _():
            col_land(core, i)
            begin(col_sends(i))

    def col_side(i):
        @pl.when((i >= 0) & (i < col_chunks))
        def _():
            col_land(1 - core, i)

    lines_early = jnp.where(y > 0, jnp.where(z == 0, row_total, 1), 0)
    pl.loop(0, lines_early)(row_line)
    for index in range(tile_count):
        tile_relay(0, index)
    early = (y == 0) & (z == 0) & (x == 1)

    @pl.when(early)
    def _():
        for tile in (1, 2):
            pl.loop(0, tile_count)(functools.partial(tile_relay, tile))

    @pl.when((z == 0) & (y == 0))
    def _():
        pl.loop(0, row_total)(row_line)

        @pl.loop(0, cands * skipped)
        def _(j):
            row_land(x, j // skipped * per_row + j % skipped)

    @pl.when((z > 0) & (y > 0))
    def _():
        pl.loop(1, 1 + AHEAD)(row_line)

    ahead = jnp.where(y > 0, 1 + AHEAD, 0)

    @pl.when(y == 0)
    def _():
        pl.loop(0, col_chunks // 2)(col_line)

    strips = side // STRIP
    start_row = jnp.where(y > 0, ROW_PACE, ROW_START + ROW_LATER * x) + ROW_HOP * z

    def slot_of(offset):
        def slot(step):
            n = offset + step
            if offset < strips:
                for tile in (1, 2):
                    index = n - TILE_START[tile]

                    @pl.when((index >= 0) & (index < tile_count) & jnp.logical_not(early))
                    def _():
                        tile_relay(tile, index)

            @pl.when((z > 0) & (n >= start_row) & ((n - start_row) % ROW_PACE == 0))
            def _():
                row_line((n - start_row) // ROW_PACE + ahead)

            @pl.when((n == COL_START) & (y == 0))
            def _():
                pl.loop(col_chunks // 2, col_chunks)(col_line)

        return slot

    factor(
        lambda c, lo: tiles[0, c, lo : lo + BLOCK, lo:].astype(F32),
        upper0, inverse0, work, diag, done, cands, side, slot_of(0),
    )
    for c in range(cands):
        inv = inverse0[c]
        a = inv.astype(BF16)
        rest = inv - a.astype(F32)
        b = rest.astype(BF16)
        d = (rest - b.astype(F32)).astype(BF16)
        raw = tiles[1, c]
        near[c] = (mm(d, raw) + mm(b, raw) + mm(a, raw)).astype(BF16)
        work[c, :, :side] = mm_tn(near[c], near[c])
        pl.loop(0, BETWEEN)(slot_of(strips + c * BETWEEN))
    factor(
        lambda c, lo: tiles[2, c, lo : lo + BLOCK, lo:].astype(F32) - work[c, lo : lo + BLOCK, lo:side],
        upper1, inverse1, work, diag, done, cands, side, slot_of(strips + cands * BETWEEN),
    )

    reached = (2 * strips + cands * BETWEEN - 1 - start_row) // ROW_PACE + 1 + ahead

    @pl.when(z > 0)
    def _():
        pl.loop(reached, row_total)(row_line)

    @pl.when(y > 0)
    def _():
        pl.loop(0, col_chunks)(col_line)

    pl.loop(0, row_total)(row_side)
    pl.loop(0, col_chunks)(col_side)

    for index in range(tile_count):
        finish(tile_sends(0, index))
    for tile in (1, 2):
        pl.loop(0, tile_count)(lambda index, tile=tile: finish(tile_sends(tile, index)))

    def flushed(k, i):
        pltpu.make_async_copy(rows.at[k, i], row_target(k, i), row_flush.at[k, i]).wait()

    @pl.loop(0, row_total)
    def _(j):
        finish(row_sends(chunk_of(j)))
        for k in range(FACTORED):
            flushed(k, chunk_of(j))

    @pl.when((z == 0) & (y == 0))
    def _():
        @pl.loop(0, cands * skipped)
        def _(j):
            flushed(x, j // skipped * per_row + j % skipped)

    @pl.loop(0, col_chunks)
    def _(i):
        finish(col_sends(i))
        for k in range(FACTORED):
            pltpu.make_async_copy(cols.at[k, i], col_target(k, i), col_flush.at[k, i]).wait()


def head(prows, pcols, side, base):
    cands, row_count, columns = base.shape
    square = jax.ShapeDtypeStruct((cands, side, side), F32)
    vmem = pl.BlockSpec(memory_space=pltpu.VMEM)
    hbm = pl.BlockSpec(memory_space=pl.ANY)
    dma = pltpu.SemaphoreType.DMA
    row_chunks = cands * row_count // BLOCK
    col_chunks = cands * side // BLOCK
    count = cands * side // BLOCK
    return pl.pallas_call(
        functools.partial(head_kernel, prows, pcols),
        out_shape=(
            square, square, square, square, jax.ShapeDtypeStruct((cands, side, side), BF16),
            jax.ShapeDtypeStruct((FACTORED, cands, row_count, side), BF16),
            jax.ShapeDtypeStruct((FACTORED, cands, side, columns), BF16),
        ),
        in_specs=[hbm],
        out_specs=(vmem,) * 5 + (hbm, hbm),
        scratch_shapes=[
            pltpu.VMEM((cands, side, 2 * side), F32),
            pltpu.VMEM((cands, BLOCK, 2 * BLOCK), F32),
            pltpu.VMEM((cands, BLOCK, 2 * BLOCK), F32),
            pltpu.VMEM((len(TILES), cands, side, side), BF16),
            pltpu.VMEM((FACTORED, row_chunks, BLOCK, side), BF16),
            pltpu.VMEM((FACTORED, col_chunks, BLOCK, columns), BF16),
            dma((len(TILES), count)), dma((len(TILES), count, 4)),
            dma((FACTORED, row_chunks)), dma((2, row_chunks)),
            dma((FACTORED, col_chunks)), dma((2, col_chunks)),
            dma((FACTORED, row_chunks)), dma((FACTORED, col_chunks)),
        ],
        compiler_params=pltpu.CompilerParams(collective_id=0, has_side_effects=True, vmem_limit_bytes=60 << 20),
        cost_estimate=pl.CostEstimate(flops=40_000_000_000, bytes_accessed=1 << 25, transcendentals=0),
        name="head",
    )(base)


def tail_kernel(prows, pcols, place, base, rows_ref, cols_ref, upper0, upper1, inv0, inv1, near, out, cols, parts):
    side = inv0.shape[-1]
    half = side // 2
    columns = base.shape[-1]
    block = pl.program_id(1)
    p, q = place[0], place[1]
    tile = block * ROWS // side * prows + p

    @pl.when(block == 0)
    def _():
        for index, inv in enumerate((inv0, inv1)):
            high, low = split(inv[0])
            parts[2 * index] = high
            parts[2 * index + 1] = low
        for index in range(columns // side):
            at = slice(index * side, (index + 1) * side)
            column = index * pcols + q
            raw = cols_ref[0, 0, :, at]
            solved = mm(parts[0], raw) + mm(parts[1], raw)
            first = jnp.where(column > 0, solved, 0.0).astype(BF16)
            cols[:side, at] = first
            rest = cols_ref[1, 0, :, at].astype(F32) - lax.dot_general(
                near[0], first, (((0,), (0,)), ((), ())), preferred_element_type=F32)
            high, low = split(rest)
            solved = mm(parts[2], high) + (mm(parts[3], high) + mm(parts[2], low))
            cols[side:, at] = jnp.where(column > 1, solved, 0.0).astype(BF16)

    def solve(pairs):
        left = sum(mm_nt(a[:, :half], b[:half, :half]) for a, b in pairs)
        right = sum(mm_nt(a, b[half:, :]) for a, b in pairs)
        return jnp.concatenate([left, right], axis=1)

    raw = rows_ref[0, 0]
    solved0 = solve([(raw, parts[0]), (raw, parts[1])])
    solved0 = jnp.where(tile > 0, solved0, 0.0)
    first = solved0.astype(BF16)
    rest = rows_ref[1, 0].astype(F32) - mm(first, near[0])
    high, low = split(rest)
    solved1 = solve([(high, parts[2]), (high, parts[3]), (low, parts[2])])
    solved1 = jnp.where(tile > 1, solved1, 0.0)
    second = solved1.astype(BF16)
    wide = columns // LANES
    rows = pl.ds(pl.multiple_of(lax.rem(block * ROWS, side), ROWS), ROWS)

    def store(value, start):
        for lane in range(value.shape[1] // LANES):
            out[pl.ds(start // LANES + lane, ROWS, stride=wide), :] = value[:, lane * LANES : (lane + 1) * LANES]

    def trail(start):
        at = slice(start, start + half)
        value = base[0, :, at].astype(F32) - (mm(first, cols[:side, at]) + mm(second, cols[side:, at]))
        store(jnp.where(tile > 1, value, 0.0), start)

    for start in range(side, columns, half):
        trail(start)

    @pl.when(q > 1)
    def _():
        for start in range(0, side, half):
            trail(start)

    for k, (solved, upper) in enumerate(((solved0, upper0), (solved1, upper1))):
        @pl.when(q == k)
        def _():
            store(solved, 0)

            @pl.when(tile == k)
            def _():
                store(upper[0, :, rows].T, 0)


def tail(prows, pcols, place, base, rows_in, cols_in, upper0, upper1, inv0, inv1, near):
    cands, rows, columns = base.shape
    side = inv0.shape[-1]
    whole = lambda a: pl.BlockSpec((1,) + a.shape[1:], lambda c, b, s: (c, 0, 0))
    part = lambda a: pl.BlockSpec((1, ROWS, a.shape[2]), lambda c, b, s: (c, b, 0))
    wide = columns // LANES
    return pl.pallas_call(
        functools.partial(tail_kernel, prows, pcols),
        out_shape=jax.ShapeDtypeStruct((cands * rows * wide, LANES), F32),
        grid_spec=pltpu.PrefetchScalarGridSpec(
            num_scalar_prefetch=1,
            grid=(cands, rows // ROWS),
            in_specs=[
                part(base),
                pl.BlockSpec((FACTORED, 1, ROWS, side), lambda c, b, s: (0, c, b, 0)),
                pl.BlockSpec((FACTORED, 1, side, columns), lambda c, b, s: (0, c, 0, 0)),
            ]
            + [whole(a) for a in (upper0, upper1, inv0, inv1, near)],
            out_specs=pl.BlockSpec((ROWS * wide, LANES), lambda c, b, s: (c * (rows // ROWS) + b, 0)),
            scratch_shapes=[pltpu.VMEM((2 * side, columns), BF16), pltpu.VMEM((4, side, side), BF16)],
        ),
        cost_estimate=pl.CostEstimate(flops=2 * cands * rows * columns * 2 * side, bytes_accessed=cands * rows * columns * 6, transcendentals=0),
        name="tail",
    )(place, base, rows_in, cols_in, upper0, upper1, inv0, inv1, near)


def shards(covariance):
    cands, row_tiles, _, side, column_tiles = covariance.shape[:5]
    prows = lax.axis_size("prow")
    pcols = lax.axis_size("pcol")
    place = jnp.stack([lax.axis_index("prow"), lax.axis_index("pcol")]).astype(jnp.int32)
    base = covariance.reshape(cands, row_tiles * side, column_tiles * side)
    upper0, inverse0, upper1, inverse1, near, rows, cols = head(prows, pcols, side, base)
    out = tail(prows, pcols, place, base, rows, cols, upper0, upper1, inverse0, inverse1, near)
    return out.reshape(covariance.shape)


def solution(mesh):
    placed = P(None, None, "prow", None, None, "pcol", None)
    return jax.shard_map(
        shards, mesh=mesh, in_specs=(placed,), out_specs=placed, check_vma=False
    )
```

```python
import functools

import jax
import jax.numpy as jnp
from jax import lax
from jax.experimental import pallas as pl
from jax.experimental.pallas import tpu as pltpu
from jax.sharding import PartitionSpec as P

FACTORED = 2
ROW_START, ROW_LATER, ROW_HOP, ROW_PACE, AHEAD = 4, 15, 2, 3, 2
COL_START, BETWEEN, LATE = 26, 4, 18
TILE_START = (0, 5, 17)
BLOCK = 128
STRIP = 16
HALF = 8
LANES = 128
ROWS = 256
TILES = ((0, 0), (0, 1), (1, 1))
MESH = pl.DeviceIdType.MESH
F32 = jnp.float32
BF16 = jnp.bfloat16


def mm(a, b):
    return jnp.dot(a, b, preferred_element_type=F32)


def mm_nt(a, b):
    return lax.dot_general(a, b, (((1,), (1,)), ((), ())), preferred_element_type=F32)


def mm_tn(a, b):
    return lax.dot_general(a, b, (((0,), (0,)), ((), ())), preferred_element_type=F32)


def split(value):
    high = value.astype(BF16)
    return high, (value - high.astype(F32)).astype(BF16)


def thirds(value):
    a = value.astype(BF16)
    rest = value - a.astype(F32)
    b = rest.astype(BF16)
    return a, b, (rest - b.astype(F32)).astype(BF16)


def dot6(left, right, turned=False):
    a, b, c = thirds(left)
    d, e, f = thirds(right)
    lefts = jnp.concatenate([a, a, b, a, c, b], 0 if turned else 1)
    rights = jnp.concatenate([d, e, d, f, d, e], 0)
    return (mm_tn if turned else mm)(lefts, rights)


def row_of(value, index):
    return jnp.broadcast_to(value[index : index + 1], value.shape)


def small_inverse(columns):
    n = len(columns)
    d = [[row_of(columns[t], i) if i >= t else None for t in range(n)] for i in range(n)]
    m = [[None] * n for _ in range(n)]
    sums = [[None] * n for _ in range(n)]
    for t in range(n):
        scale = lax.rsqrt(d[t][t])
        for j in range(t):
            m[t][j] = -(scale * sums[t][j])
        m[t][t] = scale
        for i in range(t + 1, n):
            d[i][t] = d[i][t] * scale
        for i in range(t + 1, n):
            for j in range(t + 1, i + 1):
                d[i][j] = d[i][j] - d[i][t] * d[j][t]
        for i in range(t + 1, n):
            for j in range(t + 1):
                term = d[i][t] * m[t][j]
                sums[i][j] = term if sums[i][j] is None else sums[i][j] + term
    return m


def factor(load, upper_ref, inverse_ref, work, diag, done_ref, cands, side, slot):
    blocks = side // BLOCK
    strips_per_block = BLOCK // STRIP
    eye_row = lax.broadcasted_iota(jnp.int32, (BLOCK, BLOCK), 0)
    eye_col = lax.broadcasted_iota(jnp.int32, (BLOCK, BLOCK), 1)
    eye = (eye_row == eye_col).astype(F32)
    sub = lax.broadcasted_iota(jnp.int32, (HALF, BLOCK), 0)
    each = range(cands)
    for c in each:
        work[c, :, side:] = jnp.zeros((side, side), F32)
        for block in range(blocks):
            lo = block * BLOCK
            if lo:
                work[c, lo : lo + BLOCK, :lo] = jnp.zeros((BLOCK, lo), F32)
            work[c, lo : lo + BLOCK, lo:side] = load(c, lo)
            work[c, lo : lo + BLOCK, side + lo : side + lo + BLOCK] = eye

    def spread(value, start):
        return [jnp.broadcast_to(value[:, start + t : start + t + 1], (HALF, BLOCK)) for t in range(HALF)]

    def apply(m, rows):
        out = None
        for j in range(HALF):
            column = m[j][j] if j == 0 else jnp.where(sub == j, m[j][j], 0.0)
            for i in range(j + 1, HALF):
                column = jnp.where(sub == i, m[i][j], column)
            term = jnp.concatenate([column, column], axis=1) * row_of(rows, j)
            out = term if out is None else out + term
        return out

    for block in range(blocks):
        lo = block * BLOCK
        hi = lo + BLOCK
        for c in each:
            diag[c, :, :BLOCK] = work[c, lo:hi, lo:hi]
            diag[c, :, BLOCK:] = eye

        def strip_step(step, carry):
            slot(block * strips_per_block + step)
            start = pl.multiple_of(step * STRIP, STRIP)
            shift = lax.rem(BLOCK - start, BLOCK)
            top = [diag[c, pl.ds(start, HALF), :] for c in each]
            low = [diag[c, pl.ds(start + HALF, HALF), :] for c in each]
            top_columns = [spread(pltpu.roll(top[c][:, :BLOCK], shift, 1), 0) for c in each]
            low_columns = [spread(pltpu.roll(low[c][:, :BLOCK], shift, 1), 0) for c in each]
            m = [small_inverse(top_columns[c]) for c in each]
            first = [apply(m[c], top[c]) for c in each]
            rest = []
            for c in each:
                value = low[c]
                for j in range(HALF):
                    left = sum(m[c][j][t] * low_columns[c][t] for t in range(j + 1))
                    value = value - jnp.concatenate([left, left], axis=1) * row_of(first[c], j)
                rest.append(value)
            last_columns = [spread(pltpu.roll(rest[c][:, :BLOCK], shift, 1), HALF) for c in each]
            m = [small_inverse(last_columns[c]) for c in each]
            second = [apply(m[c], rest[c]) for c in each]
            for c in each:
                both = jnp.concatenate([first[c], second[c]], axis=0)
                done_ref[c, pl.ds(start, STRIP), :] = both
                diag[c] = diag[c] - dot6(both[:, :BLOCK], both, turned=True)
            return carry

        lax.fori_loop(0, strips_per_block, strip_step, 0)
        for c in each:
            small = jnp.where(eye_row >= eye_col, done_ref[c, :, BLOCK:], 0.0)
            done = dot6(small, work[c, lo:hi, lo : side + hi])
            upper_ref[c, lo:hi, lo:side] = done[:, : side - lo]
            upper_ref[c, lo:hi, lo:hi] = jnp.where(eye_row <= eye_col, done_ref[c, :, :BLOCK], 0.0)
            if lo:
                upper_ref[c, lo:hi, :lo] = jnp.zeros((BLOCK, lo), F32)
            inverse_ref[c, lo:hi, :hi] = done[:, side - lo :]
            if hi < side:
                inverse_ref[c, lo:hi, hi:] = jnp.zeros((BLOCK, side - hi), F32)
                work[c, hi:, hi : side + hi] = work[c, hi:, hi : side + hi] - dot6(
                    done[:, BLOCK : side - lo], done[:, BLOCK:], turned=True
                )


def head_kernel(
    prows, pcols, base, upper0, upper1, cols_out, rows_out, panel_out,
    work, diag, done, tiles, rows, cols, inverse0, inverse1, near, parts, rounded, panel,
    tile_recv, tile_send, row_recv, row_send, col_recv, col_send, store_sem,
):
    cands, side = upper0.shape[:2]
    blocks = side // BLOCK
    p, q = lax.axis_index("prow"), lax.axis_index("pcol")
    y, core, z, x = p // 2, p % 2, q // 2, q % 2
    lines, planes = pcols // 2, prows // 2
    row_chunks, row_size = rows.shape[1:3]
    col_chunks, col_size = cols.shape[1:3]
    per_row = row_chunks // cands
    per_col = col_chunks // cands

    def at(dy=None, dcore=None, dz=None, dx=None):
        pick = lambda new, old: old if new is None else new
        return {
            "prow": pick(dy, y) * 2 + pick(dcore, core),
            "pcol": pick(dz, z) * 2 + pick(dx, x),
        }

    barrier = pltpu.get_barrier_semaphore()
    for target in (
        at(dy=(y + 1) % planes), at(dy=(y + planes - 1) % planes), at(dcore=1 - core),
        at(dz=(z + 1) % lines), at(dz=(z + lines - 1) % lines), at(dx=1 - x),
    ):
        pl.semaphore_signal(barrier, inc=1, device_id=target, device_id_type=MESH)

    def tile_part(tile, index):
        c, lo = index % cands, index // cands * BLOCK
        if tile:
            return c, pl.ds(pl.multiple_of(lo, BLOCK), BLOCK), slice(0, side)
        return c, slice(lo, lo + BLOCK), slice(lo, side)

    tile_count = cands * blocks

    def row_source(i):
        start = pl.multiple_of(i % per_row * row_size, row_size)
        return base.at[i // per_row, pl.ds(start, row_size), :side]

    def col_source(i):
        start = pl.multiple_of(i % per_col * col_size, col_size)
        return base.at[i // per_col, pl.ds(start, col_size)]

    for tile, (p0, q0) in enumerate(TILES):
        @pl.when((p == p0) & (q == q0))
        def _():
            for index in range(tile_count):
                c, r, s = tile_part(tile, index)
                pltpu.make_async_copy(base.at[c, r, s], tiles.at[tile, c, r, s], tile_recv.at[tile, index]).start()

    @pl.when(z == 0)
    def _():
        @pl.loop(0, row_chunks)
        def _(i):
            pltpu.make_async_copy(row_source(i), rows.at[x, i], row_recv.at[x, i]).start()

    @pl.when(y == 0)
    def _():
        @pl.loop(0, col_chunks)
        def _(i):
            pltpu.make_async_copy(col_source(i), cols.at[core, i], col_recv.at[core, i]).start()

    pl.semaphore_wait(barrier, 6)

    def tile_sends(tile, index):
        p0, q0 = TILES[tile]
        c, r, s = tile_part(tile, index)
        ref = tiles.at[tile, c, r, s]
        even = core == 0
        line = even & (y == 0) & (x == q0)
        source = (p == p0) & (q == q0)
        partner = (y == 0) & (1 - core == p0) & (q == q0)
        options = [
            (line & (z < lines - 1), at(dz=z + 1)),
            (even & (y < planes - 1), at(dy=y + 1)),
            (line, at(dx=1 - x)),
            ((even & jnp.logical_not(partner)) | ((core == 1) & source), at(dcore=1 - core)),
        ]
        return [
            (
                condition,
                pltpu.make_async_remote_copy(
                    src_ref=ref, dst_ref=ref, send_sem=tile_send.at[tile, index, way],
                    recv_sem=tile_recv.at[tile, index], device_id=target, device_id_type=MESH,
                ),
            )
            for way, (condition, target) in enumerate(options)
        ]

    def tile_relay(tile, index):
        c, r, s = tile_part(tile, index)
        ref = tiles.at[tile, c, r, s]
        pltpu.make_async_copy(ref, ref, tile_recv.at[tile, index]).wait()
        for condition, copy in tile_sends(tile, index):
            pl.when(condition)(copy.start)

    def sends(buffer, i, k, send, recv, more, step, side_step):
        ref = buffer.at[k, i]
        copy = lambda way, target: pltpu.make_async_remote_copy(
            src_ref=ref, dst_ref=ref, send_sem=send.at[way, i], recv_sem=recv.at[k, i],
            device_id=target, device_id_type=MESH,
        )
        return [(more, copy(0, step)), (None, copy(1, side_step))]

    def row_sends(i):
        return sends(rows, i, x, row_send, row_recv, z < lines - 1, at(dz=jnp.minimum(z + 1, lines - 1)), at(dx=1 - x))

    def col_sends(i):
        return sends(cols, i, core, col_send, col_recv, y < planes - 1, at(dy=jnp.minimum(y + 1, planes - 1)), at(dcore=1 - core))

    def begin(options):
        for condition, copy in options:
            if condition is None:
                copy.start()
            else:
                pl.when(condition)(copy.start)

    def finish(options):
        for condition, copy in options:
            if condition is None:
                copy.wait_send()
            else:
                pl.when(condition)(copy.wait_send)

    def row_land(k, i):
        pltpu.make_async_copy(rows.at[k, i], rows.at[k, i], row_recv.at[k, i]).wait()

    def col_land(k, i):
        pltpu.make_async_copy(cols.at[k, i], cols.at[k, i], col_recv.at[k, i]).wait()

    skipped = (1 - jnp.minimum(y, 1)) * (side // row_size)
    stream = per_row - skipped
    row_total = cands * stream

    def chunk_of(j):
        return j // stream * per_row + skipped + j % stream

    def row_line(j):
        @pl.when((j >= 0) & (j < row_total))
        def _():
            i = chunk_of(j)
            row_land(x, i)
            begin(row_sends(i))

    def row_side(j):
        @pl.when((j >= 0) & (j < row_total))
        def _():
            row_land(1 - x, chunk_of(j))

    def col_line(i):
        @pl.when((i >= 0) & (i < col_chunks))
        def _():
            col_land(core, i)
            begin(col_sends(i))

    def col_side(i):
        @pl.when((i >= 0) & (i < col_chunks))
        def _():
            col_land(1 - core, i)

    lines_early = jnp.where(y > 0, jnp.where(z == 0, row_total, 1), 0)
    pl.loop(0, lines_early)(row_line)
    for index in range(tile_count):
        tile_relay(0, index)
    early = (y == 0) & (z == 0) & (x == 1)

    @pl.when(early)
    def _():
        for tile in (1, 2):
            pl.loop(0, tile_count)(functools.partial(tile_relay, tile))

    late = early & (core == 1)

    @pl.when((z == 0) & (y == 0))
    def _():
        pl.loop(0, jnp.where(late, 0, row_total))(row_line)

        @pl.loop(0, cands * skipped)
        def _(j):
            row_land(x, j // skipped * per_row + j % skipped)

    @pl.when((z > 0) & (y > 0))
    def _():
        pl.loop(1, 1 + AHEAD)(row_line)

    ahead = jnp.where(y > 0, 1 + AHEAD, 0)

    strips = side // STRIP
    start_row = jnp.where(y > 0, ROW_PACE, ROW_START + ROW_LATER * x) + ROW_HOP * z

    def slot_of(offset):
        def slot(step):
            n = offset + step
            if offset < strips:
                for tile in (1, 2):
                    index = n - TILE_START[tile]

                    @pl.when((index >= 0) & (index < tile_count) & jnp.logical_not(early))
                    def _():
                        tile_relay(tile, index)

            @pl.when((z > 0) & (n >= start_row) & ((n - start_row) % ROW_PACE == 0))
            def _():
                row_line((n - start_row) // ROW_PACE + ahead)

            @pl.when((n == LATE) & late)
            def _():
                pl.loop(0, row_total)(row_line)

            @pl.when((n == COL_START) & (y == 0))
            def _():
                pl.loop(0, col_chunks)(col_line)

        return slot

    factor(
        lambda c, lo: tiles[0, c, lo : lo + BLOCK, lo:].astype(F32),
        upper0, inverse0, work, diag, done, cands, side, slot_of(0),
    )
    for c in range(cands):
        inv = inverse0[c]
        a = inv.astype(BF16)
        rest = inv - a.astype(F32)
        b = rest.astype(BF16)
        d = (rest - b.astype(F32)).astype(BF16)
        raw = tiles[1, c]
        near[c] = (mm(d, raw) + mm(b, raw) + mm(a, raw)).astype(BF16)
        work[c, :, :side] = mm_tn(near[c], near[c])
        pl.loop(0, BETWEEN)(slot_of(strips + c * BETWEEN))
    factor(
        lambda c, lo: tiles[2, c, lo : lo + BLOCK, lo:].astype(F32) - work[c, lo : lo + BLOCK, lo:side],
        upper1, inverse1, work, diag, done, cands, side, slot_of(strips + cands * BETWEEN),
    )

    reached = (2 * strips + cands * BETWEEN - 1 - start_row) // ROW_PACE + 1 + ahead

    @pl.when(y > 0)
    def _():
        pl.loop(0, col_chunks)(col_line)

    pl.loop(0, col_chunks)(col_side)
    for c in range(cands):
        for index, inverse in enumerate((inverse0, inverse1)):
            high, low = split(inverse[c])
            parts[c, 2 * index] = high
            parts[c, 2 * index + 1] = low

    columns = cols.shape[3]

    @pl.loop(0, cands)
    def _(c):
        for index in range(columns // side):
            place = slice(index * side, (index + 1) * side)
            column = index * pcols + q
            raw = [cols[k, pl.ds(c * per_col, per_col), :, place].reshape(side, side) for k in range(FACTORED)]
            solved = mm(parts[c, 0], raw[0]) + mm(parts[c, 1], raw[0])
            first = jnp.where(column > 0, solved, 0.0).astype(BF16)
            cols_out[0, c, :, place] = first
            high, low = split(raw[1].astype(F32) - mm_tn(near[c], first))
            solved = mm(parts[c, 2], high) + (mm(parts[c, 3], high) + mm(parts[c, 2], low))
            cols_out[1, c, :, place] = jnp.where(column > 1, solved, 0.0).astype(BF16)

    half = side // 2

    def solve(pairs):
        left = sum(mm_nt(a[:, :half], b[:half, :half]) for a, b in pairs)
        right = sum(mm_nt(a, b[half:, :]) for a, b in pairs)
        return jnp.concatenate([left, right], axis=1)

    units = cands * per_row * row_size // ROWS
    unit_chunks = ROWS // row_size

    def unit_copies(u):
        c = u * unit_chunks // per_row
        start = pl.multiple_of(u * unit_chunks % per_row * row_size, ROWS)
        turn = u % 2
        return [
            pltpu.make_async_copy(rounded.at[turn], rows_out.at[:, c, pl.ds(start, ROWS)], store_sem.at[turn, 0]),
            pltpu.make_async_copy(panel.at[turn], panel_out.at[c, pl.ds(start, ROWS)], store_sem.at[turn, 1]),
        ]

    def passed(u):
        i = u * unit_chunks
        need = i // per_row * stream + jnp.maximum(i % per_row - skipped, 0)
        return jnp.minimum(row_total, jnp.maximum(reached + u, need))

    @pl.loop(0, units)
    def _(u):
        @pl.when(z > 0)
        def _():
            pl.loop(passed(u), passed(u + 1))(row_line)

        for step in range(unit_chunks):
            i = u * unit_chunks + step
            pl.when(i % per_row >= skipped)(functools.partial(row_land, 1 - x, i))

        @pl.when(u >= 2)
        def _():
            for copy in unit_copies(u - 2):
                copy.wait()

        c = u * unit_chunks // per_row
        tile = u * unit_chunks % per_row * row_size // side * prows + p
        turn = u % 2
        raw = [rows[k, pl.ds(u * unit_chunks, unit_chunks)].reshape(ROWS, side) for k in range(FACTORED)]
        solved0 = jnp.where(tile > 0, solve([(raw[0], parts[c, 0]), (raw[0], parts[c, 1])]), 0.0)
        first = solved0.astype(BF16)
        rounded[turn, 0] = first
        high, low = split(raw[1].astype(F32) - mm(first, near[c]))
        solved1 = solve([(high, parts[c, 2]), (high, parts[c, 3]), (low, parts[c, 2])])
        solved1 = jnp.where(tile > 1, solved1, 0.0)
        rounded[turn, 1] = solved1.astype(BF16)
        panel[turn] = jnp.where(q == 0, solved0, solved1)
        for copy in unit_copies(u):
            copy.start()

    for u in range(units - 2, units):
        for copy in unit_copies(u):
            copy.wait()

    for index in range(tile_count):
        finish(tile_sends(0, index))
    for tile in (1, 2):
        pl.loop(0, tile_count)(lambda index, tile=tile: finish(tile_sends(tile, index)))

    @pl.loop(0, row_total)
    def _(j):
        finish(row_sends(chunk_of(j)))

    @pl.loop(0, col_chunks)
    def _(i):
        finish(col_sends(i))


def head(prows, pcols, side, base):
    cands, row_count, columns = base.shape
    square = jax.ShapeDtypeStruct((cands, side, side), F32)
    vmem = pl.BlockSpec(memory_space=pltpu.VMEM)
    hbm = pl.BlockSpec(memory_space=pl.ANY)
    dma = pltpu.SemaphoreType.DMA
    row_chunks = cands * row_count // BLOCK
    col_chunks = cands * side // BLOCK
    count = cands * side // BLOCK
    return pl.pallas_call(
        functools.partial(head_kernel, prows, pcols),
        out_shape=(
            square, square,
            jax.ShapeDtypeStruct((FACTORED, cands, side, columns), BF16),
            jax.ShapeDtypeStruct((FACTORED, cands, row_count, side), BF16),
            jax.ShapeDtypeStruct((cands, row_count, side), F32),
        ),
        in_specs=[hbm],
        out_specs=(vmem,) * 3 + (hbm, hbm),
        scratch_shapes=[
            pltpu.VMEM((cands, side, 2 * side), F32),
            pltpu.VMEM((cands, BLOCK, 2 * BLOCK), F32),
            pltpu.VMEM((cands, BLOCK, 2 * BLOCK), F32),
            pltpu.VMEM((len(TILES), cands, side, side), BF16),
            pltpu.VMEM((FACTORED, row_chunks, BLOCK, side), BF16),
            pltpu.VMEM((FACTORED, col_chunks, BLOCK, columns), BF16),
            pltpu.VMEM((cands, side, side), F32),
            pltpu.VMEM((cands, side, side), F32),
            pltpu.VMEM((cands, side, side), BF16),
            pltpu.VMEM((cands, 4, side, side), BF16),
            pltpu.VMEM((2, FACTORED, ROWS, side), BF16),
            pltpu.VMEM((2, ROWS, side), F32),
            dma((len(TILES), count)), dma((len(TILES), count, 4)),
            dma((FACTORED, row_chunks)), dma((2, row_chunks)),
            dma((FACTORED, col_chunks)), dma((2, col_chunks)),
            dma((2, 2)),
        ],
        compiler_params=pltpu.CompilerParams(collective_id=0, has_side_effects=True, vmem_limit_bytes=60 << 20),
        cost_estimate=pl.CostEstimate(flops=40_000_000_000, bytes_accessed=1 << 25, transcendentals=0),
        name="head",
    )(base)


def tail_kernel(prows, place, base, rows_ref, cols_ref, panel, upper0, upper1, out):
    side = upper0.shape[-1]
    half = side // 2
    columns = base.shape[-1]
    block = pl.program_id(1)
    p, q = place[0], place[1]
    tile = block * ROWS // side * prows + p
    wide = columns // LANES
    rows = pl.ds(pl.multiple_of(lax.rem(block * ROWS, side), ROWS), ROWS)
    first, second = rows_ref[0, 0], rows_ref[1, 0]

    def store(value, start):
        for lane in range(value.shape[1] // LANES):
            out[pl.ds(start // LANES + lane, ROWS, stride=wide), :] = value[:, lane * LANES : (lane + 1) * LANES]

    def trail(start):
        at = slice(start, start + half)
        value = base[0, :, at].astype(F32) - (mm(first, cols_ref[0, 0, :, at]) + mm(second, cols_ref[1, 0, :, at]))
        store(jnp.where(tile > 1, value, 0.0), start)

    for start in range(side, columns, half):
        trail(start)

    @pl.when(q > 1)
    def _():
        for start in range(0, side, half):
            trail(start)

    @pl.when(q < FACTORED)
    def _():
        store(panel[0], 0)

    for k, upper in enumerate((upper0, upper1)):
        @pl.when((q == k) & (tile == k))
        def _():
            store(upper[0, :, rows].T, 0)


def tail(prows, place, base, rows_in, cols_in, panel, upper0, upper1):
    cands, rows, columns = base.shape
    side = upper0.shape[-1]
    wide = columns // LANES
    square = pl.BlockSpec((1, side, side), lambda c, b, s: (c, 0, 0))
    return pl.pallas_call(
        functools.partial(tail_kernel, prows),
        out_shape=jax.ShapeDtypeStruct((cands * rows * wide, LANES), F32),
        grid_spec=pltpu.PrefetchScalarGridSpec(
            num_scalar_prefetch=1,
            grid=(cands, rows // ROWS),
            in_specs=[
                pl.BlockSpec((1, ROWS, columns), lambda c, b, s: (c, b, 0)),
                pl.BlockSpec((FACTORED, 1, ROWS, side), lambda c, b, s: (0, c, b, 0)),
                pl.BlockSpec((FACTORED, 1, side, columns), lambda c, b, s: (0, c, 0, 0)),
                pl.BlockSpec((1, ROWS, side), lambda c, b, s: (c, b, 0)),
                square,
                square,
            ],
            out_specs=pl.BlockSpec((ROWS * wide, LANES), lambda c, b, s: (c * (rows // ROWS) + b, 0)),
        ),
        cost_estimate=pl.CostEstimate(
            flops=2 * cands * rows * columns * 2 * side, bytes_accessed=cands * rows * columns * 6, transcendentals=0
        ),
        name="tail",
    )(place, base, rows_in, cols_in, panel, upper0, upper1)


def shards(covariance):
    cands, row_tiles, _, side, column_tiles = covariance.shape[:5]
    prows = lax.axis_size("prow")
    pcols = lax.axis_size("pcol")
    place = jnp.stack([lax.axis_index("prow"), lax.axis_index("pcol")]).astype(jnp.int32)
    base = covariance.reshape(cands, row_tiles * side, column_tiles * side)
    upper0, upper1, cols, rows, panel = head(prows, pcols, side, base)
    out = tail(prows, place, base, rows, cols, panel, upper0, upper1)
    return out.reshape(covariance.shape)


def solution(mesh):
    placed = P(None, None, "prow", None, None, "pcol", None)
    return jax.shard_map(
        shards, mesh=mesh, in_specs=(placed,), out_specs=placed, check_vma=False
    )
```
